512 devices in a mesh: rep: 16 (over z, core), tp: 32 (over y, x).
Axes of the slice: x: 4, y: 8, z: 8, core: 2. Of those that a mesh axis runs over, the one named last changes fastest.
Arguments:
- attn: bfloat16 [12288, 4096], P('rep', 'tp'), parts along dimension 0, may hold values from -6 to 6
- output_weight: bfloat16 [4096, 8192], P(None, 'tp'), may hold values from -0.09375 to 0.09375
- adapter_down_weight: bfloat16 [32, 64, 4096], P('tp'), may hold values from -0.09375 to 0.09375
- adapter_up_weight: bfloat16 [32, 64, 8192], P('tp'), may hold values from -0.75 to 0.75
- block_adapter_index: int32 [96], P('rep'), parts along dimension 0, may hold values from 0 to 31
- adapter_page_table: int32 [32], replicated, may hold values from 0 to 31, each once
Outputs:
- projected: bfloat16 [12288, 8192], P('rep', 'tp'), parts along dimension 0
The draws below stay inside these ranges and needn't reach their ends.
There are 16 independent parts, one for each index of `rep`. The reference program is written for one: setup_inputs(seed, part) draws one part's arguments, and reference() takes and returns one part's arrays. A program takes and returns all parts, laid end to end along the dimension named above; an argument that names none is the same for every part. Nothing has to cross between parts.
Inputs may be any that keep to these rules, and one draw needn't show every extreme that they name: adapter_page_table is a permutation; adapter a is stored on tp device adapter_page_table[a] (each device holds exactly one adapter), and row adapter_page_table[a] of adapter_down_weight and adapter_up_weight holds it. `block_adapter_index`: the adapter used by all 128 tokens of a block.
All inputs are finite; a program needn't handle non-finite values.
Results may differ from the reference program's by a relative error of at most 0.0046.
Values may be sent and summed in bfloat16 or wider, within the bound.
No kernel may reach another device: no remote copies, remote signals or barrier semaphores. Data moves between devices by JAX's collectives and lax.ppermute only.
A program may use at most 64 MiB of HBM per device.

```python
import jax
import jax.numpy as jnp
from jax import lax

MODEL_WIDTH = 8192
ADAPTER_RANK = 64
BLOCK = 128
TOKENS = 768
ATTN_FEATURES = 4096
ADAPTER_COUNT = 32
BLOCKS = 6


def place_ends(array, own_key, least, high):
    index_at = [jax.random.randint(jax.random.fold_in(own_key, axis), (), 0, length) for axis, length in enumerate(array.shape)]
    longest = array.shape.index(max(array.shape))
    neighbour = index_at[:longest] + [(index_at[longest] + 1) % array.shape[longest]] + index_at[longest + 1:]
    return array.at[tuple(index_at)].set(least).at[tuple(neighbour)].set(high)


def levels(own_key, extent, shards, smallest, high):
    gain, own = 1.0, jax.random.fold_in(own_key, 6)
    for position, blocks in shards:
        steps = jnp.exp(jax.random.uniform(jax.random.fold_in(own, position), (blocks,), jnp.float32, smallest / len(shards), high / len(shards)))
        gain = gain * jnp.repeat(steps, extent[position] // blocks).reshape([-1 if axis == position else 1 for axis in range(len(extent))])
    return gain


def noise(own_key, shape, deviation, reach, cuts=(), held_as=jnp.bfloat16):
    drawn = jax.random.normal(own_key, shape, jnp.float32) * deviation
    if len(cuts) > 0:
        drawn = levels(own_key, shape, cuts, -0.22, 0.18) * drawn
    return jnp.clip(drawn, min=-reach, max=reach).astype(held_as)


def setup_inputs(seed: int = 0, part: int = 0) -> dict:
    key_list = jax.random.split(jax.random.key(seed), 7)
    own_keys = jax.random.split(jax.random.fold_in(key_list[6], part), 7)
    attn = noise(own_keys[0], (TOKENS, ATTN_FEATURES), 1.0, 6.0, ((1, 32),))
    output_weight = noise(key_list[1], (ATTN_FEATURES, MODEL_WIDTH), ATTN_FEATURES ** -0.5, 0.09375, ((1, 32),))
    adapter_down_weight = noise(key_list[2], (ADAPTER_COUNT, ADAPTER_RANK, ATTN_FEATURES), ATTN_FEATURES ** -0.5, 0.09375, ((0, 32),))
    adapter_up_weight = noise(key_list[3], (ADAPTER_COUNT, ADAPTER_RANK, MODEL_WIDTH), ADAPTER_RANK ** -0.5, 0.75, ((0, 32),))
    block_adapter_index = place_ends(jax.random.randint(own_keys[4], (BLOCKS,), 0, ADAPTER_COUNT), jax.random.fold_in(own_keys[4], 1), 0, ADAPTER_COUNT - 1).astype(jnp.int32)
    adapter_page_table = jax.random.permutation(key_list[5], ADAPTER_COUNT).astype(jnp.int32)
    return {"attn": attn, "output_weight": output_weight, "adapter_down_weight": adapter_down_weight, "adapter_up_weight": adapter_up_weight, "block_adapter_index": block_adapter_index, "adapter_page_table": adapter_page_table}


adapter_scale = 2.0


def reference(attn, output_weight, adapter_down_weight, adapter_up_weight, block_adapter_index, adapter_page_table):
    block_page_index = adapter_page_table[block_adapter_index].astype(jnp.int32)
    base_output = jnp.dot(attn, output_weight, preferred_element_type=jnp.float32)
    row_blocks = attn.reshape(BLOCKS, BLOCK, ATTN_FEATURES).astype(jnp.float32)
    down_block_rows = adapter_down_weight[block_page_index].astype(jnp.float32)
    shrunk = jnp.einsum("btf,brf->brt", row_blocks, down_block_rows, precision=lax.Precision.HIGHEST)
    shrunk_low = lax.optimization_barrier(shrunk.astype(jnp.bfloat16))
    up_block_rows = adapter_up_weight[block_page_index].astype(jnp.float32)
    adapter_output = jnp.einsum("brt,brc->btc", shrunk_low.astype(jnp.float32), up_block_rows, precision=lax.Precision.HIGHEST)
    adapter_output = adapter_output.reshape(TOKENS, MODEL_WIDTH)
    return (base_output + adapter_scale * adapter_output).astype(jnp.bfloat16)
```

```python
import functools

import jax
import jax.numpy as jnp
from jax import lax
from jax.experimental import pallas as pl
from jax.experimental.pallas import tpu as pltpu
from jax.sharding import Mesh, PartitionSpec as P

RANK = 64
BLOCK = 128
NY, PARITIES = 8, 2
CORES = 2
PIECE = 16
adapter_scale = 2.0
MIB = 1 << 20

VMEM = pl.BlockSpec(memory_space=pltpu.VMEM)
SMEM = pl.BlockSpec(memory_space=pltpu.SMEM)
ANY = pl.BlockSpec(memory_space=pl.ANY)


def cost(nbytes, flops=0):
    return pl.CostEstimate(flops=flops, transcendentals=0, bytes_accessed=nbytes)


def params(mib):
    return pltpu.CompilerParams(vmem_limit_bytes=mib * MIB)


def pack_kernel(core_ref, down_ref, up_ref, out_ref, down_half, up_half, sems):
    ranks = down_half.shape[0]
    rows = pl.ds(pl.multiple_of(core_ref[0] * ranks, ranks), ranks)
    copies = [
        pltpu.make_async_copy(down_ref.at[0, rows, :], down_half, sems.at[0]),
        pltpu.make_async_copy(up_ref.at[0, rows, :], up_half, sems.at[1]),
    ]
    for c in copies:
        c.start()
    n = out_ref.shape[0]
    own, width = down_half.shape[1] // n, up_half.shape[1] // n
    copies[0].wait()
    for d in range(n):
        out_ref[d, :, :own] = down_half[:, d * own : (d + 1) * own]
    copies[1].wait()
    for d in range(n):
        out_ref[d, :, own:] = up_half[:, d * width : (d + 1) * width]


def pack(core, down, up, tp):
    ranks = RANK // CORES
    own, width = down.shape[2] // tp, up.shape[2] // tp
    return pl.pallas_call(
        pack_kernel,
        out_shape=jax.ShapeDtypeStruct((tp, ranks, own + width), down.dtype),
        in_specs=[SMEM, ANY, ANY],
        out_specs=VMEM,
        scratch_shapes=[
            pltpu.VMEM((ranks, down.shape[2]), down.dtype),
            pltpu.VMEM((ranks, up.shape[2]), up.dtype),
            pltpu.SemaphoreType.DMA((2,)),
        ],
        compiler_params=params(8),
        cost_estimate=cost(2 * MIB),
    )(core, down, up)


def choose_kernel(index_ref, other_ref, table_ref, pages_ref, own_ref, send_ref, sems):
    n = own_ref.shape[0]
    copies = []
    for b in range(n):
        for i, (who, out) in enumerate(((other_ref, send_ref), (index_ref, own_ref))):
            page = table_ref[who[b]]
            copies.append(pltpu.make_async_copy(pages_ref.at[page], out.at[b], sems.at[i, b]))
    for c in copies:
        c.start()
    for c in copies:
        c.wait()


def choose(index, other, table, pages):
    shape = jax.ShapeDtypeStruct((index.shape[0],) + pages.shape[1:], pages.dtype)
    return pl.pallas_call(
        choose_kernel,
        out_shape=[shape, shape],
        in_specs=[SMEM, SMEM, SMEM, ANY],
        out_specs=[VMEM, VMEM],
        scratch_shapes=[pltpu.SemaphoreType.DMA((2, index.shape[0]))],
        compiler_params=params(8),
        cost_estimate=cost(MIB // 2),
    )(index, other, table, pages)


def shrink_kernel(attn_ref, mine_ref, other_ref, out_ref):
    own = attn_ref.shape[1]
    blocks = mine_ref.shape[0]
    each = RANK // PIECE
    for b in range(blocks):
        down = jnp.concatenate([mine_ref[b, :, :own], other_ref[b, :, :own]], axis=0)
        shrunk = lax.dot_general(
            down,
            attn_ref[b * BLOCK : (b + 1) * BLOCK, :],
            (((1,), (1,)), ((), ())),
            preferred_element_type=jnp.float32,
        ).astype(out_ref.dtype)
        out_ref[b * each : (b + 1) * each] = shrunk.reshape(each, PIECE, BLOCK)
    rest = out_ref.shape[0] - blocks * each
    if rest:
        out_ref[blocks * each :] = jnp.zeros((rest, PIECE, BLOCK), out_ref.dtype)


def shrink(attn, mine, other, tp):
    return pl.pallas_call(
        shrink_kernel,
        out_shape=jax.ShapeDtypeStruct((tp, PIECE, BLOCK), jnp.bfloat16),
        in_specs=[VMEM] * 3,
        out_specs=VMEM,
        compiler_params=params(8),
        cost_estimate=cost(MIB // 2, 2 * attn.size * RANK),
    )(attn, mine, other)


def total_kernel(in_ref, out_ref):
    total = jnp.sum(in_ref[...].astype(jnp.float32), axis=0)
    out_ref[...] = jnp.broadcast_to(total.astype(out_ref.dtype)[None], out_ref.shape)


def total(pieces):
    return pl.pallas_call(
        total_kernel,
        out_shape=jax.ShapeDtypeStruct(pieces.shape, pieces.dtype),
        in_specs=[VMEM],
        out_specs=VMEM,
        compiler_params=params(4),
        cost_estimate=cost(MIB // 4),
    )(pieces)


def matmul_kernel(at_ref, same, low, high, weight, w1, w2, w3, *refs):
    outs, (gathered, held, x_sems, w_sems) = refs[:4], refs[4:]
    tokens, own = same.shape[1], same.shape[2]
    n = same.shape[0]
    x, parity = at_ref[0], at_ref[1]
    nx = len(outs)
    copies = []
    for h in range(n):
        away = low.at[h] if h < n // 2 else high.at[h - n // 2]
        for i, (src, p) in enumerate(((same.at[h], parity), (away, 1 - parity))):
            to = pl.ds(pl.multiple_of((PARITIES * h + p) * own, own), own)
            copies.append(pltpu.make_async_copy(src, gathered.at[:, to], x_sems.at[i, h]))
    rows = PARITIES * n
    first = []
    for r in range(rows):
        src = weight.at[pl.ds(pl.multiple_of((r * nx + x) * own, own), own), :]
        first.append(pltpu.make_async_copy(src, held.at[0, r], w_sems.at[0, r]))
    others = [
        pltpu.make_async_copy(w, held.at[k + 1], w_sems.at[k + 1, 0]) for k, w in enumerate((w1, w2, w3))
    ]
    for c in copies + others + first:
        c.start()
    for c in copies:
        c.wait()
    for k in (1, 2, 3, 0):
        if k:
            others[k - 1].wait()
        else:
            for c in first:
                c.wait()
        w = held[k].reshape(rows * own, held.shape[3])
        for m in range(0, tokens, 256):
            outs[k][m : m + 256, :] = jnp.dot(
                gathered[m : m + 256, :], w, preferred_element_type=jnp.float32
            ).astype(outs[k].dtype)


def matmul(at, same, low, high, weight, ws):
    tokens, own = same.shape[1:]
    width = weight.shape[1]
    rows = PARITIES * same.shape[0]
    out = [
        jax.ShapeDtypeStruct((tokens, width), jnp.bfloat16 if k else jnp.float32)
        for k in range(4)
    ]
    return pl.pallas_call(
        matmul_kernel,
        out_shape=out,
        in_specs=[SMEM] + [ANY] * 7,
        out_specs=[VMEM] * 4,
        scratch_shapes=[
            pltpu.VMEM((tokens, rows * own), jnp.bfloat16),
            pltpu.VMEM((4, rows, own, width), jnp.bfloat16),
            pltpu.SemaphoreType.DMA((2, same.shape[0])),
            pltpu.SemaphoreType.DMA((4, rows)),
        ],
        compiler_params=params(16),
        cost_estimate=cost(6 * MIB, 2 * tokens * rows * own * width * 4),
    )(at, same, low, high, weight, *ws)


def last_kernel(low_ref, up_a_ref, up_b_ref, own_ref, r1_ref, r2_ref, r3_ref, out_ref):
    first = up_a_ref.shape[2] - out_ref.shape[1]
    each = RANK // PIECE
    for b in range(up_a_ref.shape[0]):
        rows = slice(b * BLOCK, (b + 1) * BLOCK)
        up = jnp.concatenate([up_a_ref[b, :, first:], up_b_ref[b, :, first:]], axis=0)
        shrunk = low_ref[b * each : (b + 1) * each].reshape(RANK, BLOCK)
        adapted = lax.dot_general(
            shrunk, up, (((0,), (0,)), ((), ())), preferred_element_type=jnp.float32
        )
        base = own_ref[rows, :]
        for r in (r1_ref, r2_ref, r3_ref):
            base = base + r[rows, :].astype(jnp.float32)
        out_ref[rows, :] = (base + adapter_scale * adapted).astype(out_ref.dtype)


def last(low, up_a, up_b, own, received):
    return pl.pallas_call(
        last_kernel,
        out_shape=jax.ShapeDtypeStruct(own.shape, jnp.bfloat16),
        in_specs=[VMEM] * 7,
        out_specs=VMEM,
        compiler_params=params(8),
        cost_estimate=cost(3 * MIB, 2 * own.size * RANK),
    )(low, up_a, up_b, own, *received)


def solution(mesh):
    tp, rep = mesh.shape["tp"], mesh.shape["rep"]
    nx = tp // NY
    names = ("z", "core", "yh", "yl", "x")
    grid = Mesh(
        mesh.devices.reshape(rep // CORES, CORES, NY // PARITIES, PARITIES, nx), names
    )
    reps, tps, ys = names[:2], names[2:], names[2:4]

    def shift(a, axis, size, by):
        return lax.ppermute(a, axis, [(i, (i + by) % size) for i in range(size)])

    def local(attn, weight, down, up, index, table):
        own, width = attn.shape[1], weight.shape[1]
        x, parity, core = (lax.axis_index(a).astype(jnp.int32) for a in ("x", "yl", "core"))

        pages = lax.all_to_all(pack(core[None], down, up, tp), tps, 0, 0, tiled=True)
        other_index = shift(index, "core", CORES, 1)

        same = lax.all_gather(attn, "yh")
        half = same.shape[0] // 2
        low_y = shift(same[:half], ys, NY, 1)
        high_y = shift(same[half:], ys, NY, -1)

        by_x = weight.reshape(NY, nx, own, width)
        ws = []
        for k in range(1, nx):
            mine = lax.dynamic_index_in_dim(by_x, (x + (nx - k)) % nx, 1, keepdims=False)
            ws.append(shift(mine, "x", nx, nx - k))

        mine, send = choose(index, other_index, table, pages)
        other = shift(send, "core", CORES, 1)
        pieces = shrink(attn, mine, other, tp)
        pieces = lax.all_to_all(pieces, tps, 0, 0, tiled=True)
        low = lax.all_to_all(total(pieces), tps, 0, 0, tiled=True)

        outs = matmul(jnp.stack([x, parity]), same, low_y, high_y, weight, ws)
        received = [shift(outs[k], "x", nx, k) for k in range(1, nx)]
        return last(low, mine, other, outs[0], received)

    return jax.shard_map(
        local,
        mesh=grid,
        in_specs=(P(reps, tps), P(None, tps), P(tps), P(tps), P(reps), P()),
        out_specs=P(reps, tps),
        check_vma=False,
    )
```

```python
import functools

import jax
import jax.numpy as jnp
from jax import lax
from jax.experimental import pallas as pl
from jax.experimental.pallas import tpu as pltpu
from jax.sharding import Mesh, PartitionSpec as P

RANK = 64
BLOCK = 128
NY, PARITIES = 8, 2
CORES = 2
PIECE = 16
adapter_scale = 2.0
MIB = 1 << 20
WHOLE = 60

VMEM = pl.BlockSpec(memory_space=pltpu.VMEM)
SMEM = pl.BlockSpec(memory_space=pltpu.SMEM)
ANY = pl.BlockSpec(memory_space=pl.ANY)


def cost(nbytes, flops=0):
    return pl.CostEstimate(flops=flops, transcendentals=0, bytes_accessed=nbytes)


def params(mib):
    return pltpu.CompilerParams(vmem_limit_bytes=mib * MIB)


def pack_kernel(down_ref, out_ref, held, sem):
    copy = pltpu.make_async_copy(down_ref.at[0], held, sem)
    copy.start()
    copy.wait()
    own = out_ref.shape[2]
    for d in range(out_ref.shape[0]):
        out_ref[d] = held[:, d * own : (d + 1) * own]


def pack(down, tp):
    return pl.pallas_call(
        pack_kernel,
        out_shape=jax.ShapeDtypeStruct((tp, RANK, down.shape[2] // tp), down.dtype),
        in_specs=[ANY],
        out_specs=VMEM,
        scratch_shapes=[pltpu.VMEM(down.shape[1:], down.dtype), pltpu.SemaphoreType.DMA],
        compiler_params=params(WHOLE),
        cost_estimate=cost(MIB),
    )(down)


def shrink_kernel(index_ref, table_ref, attn_ref, pages_ref, out_ref):
    blocks = index_ref.shape[0]
    each = RANK // PIECE
    for b in range(blocks):
        shrunk = lax.dot_general(
            pages_ref[table_ref[index_ref[b]]],
            attn_ref[b * BLOCK : (b + 1) * BLOCK, :],
            (((1,), (1,)), ((), ())),
            preferred_element_type=jnp.float32,
        ).astype(out_ref.dtype)
        out_ref[b * each : (b + 1) * each] = shrunk.reshape(each, PIECE, BLOCK)
    rest = out_ref.shape[0] - blocks * each
    if rest:
        out_ref[blocks * each :] = jnp.zeros((rest, PIECE, BLOCK), out_ref.dtype)


def shrink(index, table, attn, pages):
    return pl.pallas_call(
        shrink_kernel,
        out_shape=jax.ShapeDtypeStruct((pages.shape[0], PIECE, BLOCK), jnp.bfloat16),
        in_specs=[SMEM, SMEM, VMEM, VMEM],
        out_specs=VMEM,
        compiler_params=params(8),
        cost_estimate=cost(MIB // 2, 2 * attn.size * RANK),
    )(index, table, attn, pages)


def choose_kernel(index_ref, other_ref, table_ref, pages_ref, own_ref, send_ref, sems):
    n = own_ref.shape[0]
    copies = []
    for i, (who, out) in enumerate(((other_ref, send_ref), (index_ref, own_ref))):
        for b in range(n):
            src = pages_ref.at[table_ref[who[b]], pl.ds(PIECE, RANK), :]
            copies.append(pltpu.make_async_copy(src, out.at[b], sems.at[i, b]))
    for c in copies:
        c.start()
    for c in copies:
        c.wait()


def choose(index, other, table, pages):
    shape = jax.ShapeDtypeStruct((index.shape[0], RANK, pages.shape[2]), pages.dtype)
    return pl.pallas_call(
        choose_kernel,
        out_shape=[shape, shape],
        in_specs=[SMEM, SMEM, SMEM, ANY],
        out_specs=[VMEM, VMEM],
        scratch_shapes=[pltpu.SemaphoreType.DMA((2, index.shape[0]))],
        compiler_params=params(8),
        cost_estimate=cost(MIB // 2),
    )(index, other, table, pages)


def total_kernel(core_ref, in_ref, up_ref, out_ref, up, sem):
    ranks = up.shape[0]
    rows = pl.ds(pl.multiple_of(core_ref[0] * ranks, ranks), ranks)
    copy = pltpu.make_async_copy(up_ref.at[0, rows, :], up, sem)
    copy.start()
    summed = jnp.sum(in_ref[...].astype(jnp.float32), axis=0).astype(out_ref.dtype)
    n, _, own = out_ref.shape
    copy.wait()
    for d in range(n):
        out_ref[d, :PIECE, :] = summed
        for i in range(CORES):
            at = PIECE + i * ranks
            out_ref[d, at : at + ranks, :] = up[:, (CORES * d + i) * own : (CORES * d + i + 1) * own]


def total(core, pieces, up):
    tp, _, own = pieces.shape
    return pl.pallas_call(
        total_kernel,
        out_shape=jax.ShapeDtypeStruct((tp, PIECE + RANK, own), pieces.dtype),
        in_specs=[SMEM, VMEM, ANY],
        out_specs=VMEM,
        scratch_shapes=[pltpu.VMEM((RANK // CORES, up.shape[2]), up.dtype), pltpu.SemaphoreType.DMA],
        compiler_params=params(8),
        cost_estimate=cost(MIB),
    )(core, pieces, up)


def product_kernel(n, parts, parity_ref, x_ref, *refs):
    offsets = [o for p in parts for o in p]
    xs, weights, outs = refs[: len(parts)], refs[len(parts) : len(parts) + n], refs[len(parts) + n : len(parts) + 2 * n]
    gathered, held, x_sems, w_sems = refs[len(parts) + 2 * n :]
    parity = parity_ref[0]
    ny, own = held.shape[1], held.shape[2]
    at, copies = 0, []
    for i, (x, p) in enumerate(zip(xs, parts)):
        to = gathered.at[at] if len(x.shape) == 2 else gathered.at[pl.ds(at, len(p))]
        copies.append(pltpu.make_async_copy(x, to, x_sems.at[i]))
        at += len(p)
    into = []
    for k, w in enumerate(weights):
        if len(w.shape) == 3:
            into.append([pltpu.make_async_copy(w, held.at[k], w_sems.at[k, 0])])
        else:
            nx = w.shape[0] // (ny * own)
            into.append([])
            for r in range(ny):
                rows = pl.ds(pl.multiple_of((r * nx + x_ref[0]) * own, own), own)
                into[-1].append(pltpu.make_async_copy(w.at[rows, :], held.at[k, r], w_sems.at[k, r]))
    for c in (*copies, *[c for group in into for c in group]):
        c.start()
    for c in copies:
        c.wait()
    for k in range(n):
        for c in into[k]:
            c.wait()
        w = jnp.concatenate([held[k, o + (1 - parity if p else parity)] for p, o in offsets], axis=0)
        for m in range(0, gathered.shape[1], 256):
            rows = slice(m, m + 256)
            x = jnp.concatenate([gathered[j, rows, :] for j in range(ny)], axis=1)
            outs[k][rows, :] = jnp.dot(x, w, preferred_element_type=jnp.float32).astype(outs[k].dtype)


def product(scalars, gathered, parts, weights, dtypes):
    n = len(weights)
    tokens, own = gathered[0].shape[-2:]
    ny = sum(len(p) for p in parts)
    width = weights[0].shape[-1]
    return pl.pallas_call(
        functools.partial(product_kernel, n, parts),
        out_shape=[jax.ShapeDtypeStruct((tokens, width), d) for d in dtypes],
        in_specs=[SMEM] * 2 + [ANY] * (len(gathered) + n),
        out_specs=[VMEM] * n,
        scratch_shapes=[
            pltpu.VMEM((ny, tokens, own), gathered[0].dtype),
            pltpu.VMEM((n, ny, own, width), weights[0].dtype),
            pltpu.SemaphoreType.DMA((len(gathered),)),
            pltpu.SemaphoreType.DMA((n, ny)),
        ],
        compiler_params=params(WHOLE),
        cost_estimate=cost(2 * n * MIB, 2 * tokens * ny * own * width * n),
    )(*scalars, *gathered, *weights)


def last_kernel(core_ref, low_ref, mine_ref, other_ref, own_hbm, r1_ref, r2_ref, r3_ref, out_ref, own_ref, sem):
    copy = pltpu.make_async_copy(own_hbm, own_ref, sem)
    copy.start()
    core = core_ref[0]
    half = RANK // CORES
    each = half // PIECE
    for b in range(mine_ref.shape[0]):
        rows = slice(b * BLOCK, (b + 1) * BLOCK)
        up = jnp.concatenate(
            [
                jnp.concatenate([r[b, i * half : (i + 1) * half, :] for i in range(CORES)], axis=1)
                for r in (mine_ref, other_ref)
            ],
            axis=0,
        )
        at = b * CORES * each
        shrunk = jnp.concatenate(
            [low_ref[pl.ds(at + c * each, each), :PIECE, :].reshape(half, BLOCK) for c in (core, 1 - core)], axis=0
        )
        adapted = lax.dot_general(
            shrunk, up, (((0,), (0,)), ((), ())), preferred_element_type=jnp.float32
        )
        if b == 0:
            copy.wait()
        base = own_ref[rows, :]
        for r in (r1_ref, r2_ref, r3_ref):
            base = base + r[rows, :].astype(jnp.float32)
        out_ref[rows, :] = (base + adapter_scale * adapted).astype(out_ref.dtype)


def last(core, low, mine, other, own, received):
    return pl.pallas_call(
        last_kernel,
        out_shape=jax.ShapeDtypeStruct(own.shape, jnp.bfloat16),
        in_specs=[SMEM] + [VMEM] * 3 + [ANY] + [VMEM] * 3,
        out_specs=VMEM,
        scratch_shapes=[pltpu.VMEM(own.shape, own.dtype), pltpu.SemaphoreType.DMA],
        compiler_params=params(8),
        cost_estimate=cost(3 * MIB, 2 * own.size * RANK),
    )(core, low, mine, other, own, *received)


def solution(mesh):
    tp, rep = mesh.shape["tp"], mesh.shape["rep"]
    ny, nx = NY, tp // NY
    names = ("z", "core", "yh", "yl", "x")
    grid = Mesh(mesh.devices.reshape(rep // CORES, CORES, ny // PARITIES, PARITIES, nx), names)
    reps, tps, ys = names[:2], names[2:], names[2:4]

    def shift(a, axis, size, by):
        return lax.ppermute(a, axis, [(i, (i + by) % size) for i in range(size)])

    def local(attn, weight, down, up, index, table):
        own, width = attn.shape[1], weight.shape[1]
        x, parity, core = (lax.axis_index(a).astype(jnp.int32) for a in ("x", "yl", "core"))
        scalars = (parity[None], x[None])

        pages = lax.all_to_all(pack(down, tp), tps, 0, 0, tiled=True)

        same = lax.all_gather(attn, "yh")
        pages, same = lax.optimization_barrier((pages, same))
        half = same.shape[0] // 2
        low_y = shift(same[:half], ys, ny, 1)
        high_y = shift(same[half:], ys, ny, -1)
        gathered = (same, low_y, high_y)
        parts = tuple(
            tuple((p, PARITIES * h) for h in hs)
            for p, hs in ((0, range(2 * half)), (1, range(half)), (1, range(half, 2 * half)))
        )

        by_x = weight.reshape(ny, nx, own, width)
        ws = [
            lax.dynamic_index_in_dim(by_x, (x + (nx - k)) % nx, 1, keepdims=False)
            for k in range(1, nx)
        ]
        ws = [shift(w, "x", nx, nx - k) for k, w in enumerate(ws, 1)]

        pieces = shrink(index, table, attn, pages)
        pieces = lax.all_to_all(pieces, tps, 0, 0, tiled=True)

        *outs, mid = product(
            scalars, gathered, parts, [*ws, weight], [jnp.bfloat16] * len(ws) + [jnp.float32]
        )
        pieces = lax.optimization_barrier((pieces, outs))[0]
        summed = total(core[None], pieces, up)
        low = lax.all_to_all(summed, tps, 0, 0, tiled=True)
        received = [shift(o, "x", nx, k) for k, o in enumerate(outs, 1)]

        index, _ = lax.optimization_barrier((index, (summed, outs)))
        other_index = shift(index, "core", CORES, 1)
        mine, send = choose(index, other_index, table, low)
        other = shift(send, "core", CORES, 1)
        return last(core[None], low, mine, other, mid, received)

    return jax.shard_map(
        local,
        mesh=grid,
        in_specs=(P(reps, tps), P(None, tps), P(tps), P(tps), P(reps), P()),
        out_specs=P(reps, tps),
        check_vma=False,
    )
```

```python
import functools

import jax
import jax.numpy as jnp
from jax import lax
from jax.experimental import pallas as pl
from jax.experimental.pallas import tpu as pltpu
from jax.sharding import Mesh, PartitionSpec as P

RANK = 64
BLOCK = 128
NY, PARITIES = 8, 2
CORES = 2
PIECE = 16
adapter_scale = 2.0
MIB = 1 << 20
WHOLE = 60

VMEM = pl.BlockSpec(memory_space=pltpu.VMEM)
SMEM = pl.BlockSpec(memory_space=pltpu.SMEM)
ANY = pl.BlockSpec(memory_space=pl.ANY)


def cost(nbytes, flops=0):
    return pl.CostEstimate(flops=flops, transcendentals=0, bytes_accessed=nbytes)


def params(mib):
    return pltpu.CompilerParams(vmem_limit_bytes=mib * MIB)


def pack_kernel(down_ref, out_ref, held, sem):
    copy = pltpu.make_async_copy(down_ref.at[0], held, sem)
    copy.start()
    copy.wait()
    own = out_ref.shape[2]
    for d in range(out_ref.shape[0]):
        out_ref[d] = held[:, d * own : (d + 1) * own]


def pack(down, tp):
    return pl.pallas_call(
        pack_kernel,
        out_shape=jax.ShapeDtypeStruct((tp, RANK, down.shape[2] // tp), down.dtype),
        in_specs=[ANY],
        out_specs=VMEM,
        scratch_shapes=[pltpu.VMEM(down.shape[1:], down.dtype), pltpu.SemaphoreType.DMA],
        compiler_params=params(WHOLE),
        cost_estimate=cost(MIB),
    )(down)


def shrink_kernel(index_ref, table_ref, attn_ref, pages_ref, out_ref):
    blocks = index_ref.shape[0]
    each = RANK // PIECE
    for b in range(blocks):
        shrunk = lax.dot_general(
            pages_ref[table_ref[index_ref[b]]],
            attn_ref[b * BLOCK : (b + 1) * BLOCK, :],
            (((1,), (1,)), ((), ())),
            preferred_element_type=jnp.float32,
        ).astype(out_ref.dtype)
        out_ref[b * each : (b + 1) * each] = shrunk.reshape(each, PIECE, BLOCK)
    rest = out_ref.shape[0] - blocks * each
    if rest:
        out_ref[blocks * each :] = jnp.zeros((rest, PIECE, BLOCK), out_ref.dtype)


def shrink(index, table, attn, pages):
    return pl.pallas_call(
        shrink_kernel,
        out_shape=jax.ShapeDtypeStruct((pages.shape[0], PIECE, BLOCK), jnp.bfloat16),
        in_specs=[SMEM, SMEM, VMEM, VMEM],
        out_specs=VMEM,
        compiler_params=params(8),
        cost_estimate=cost(MIB // 2, 2 * attn.size * RANK),
    )(index, table, attn, pages)


def choose_kernel(index_ref, other_ref, table_ref, pages_ref, own_ref, send_ref, sems):
    n = own_ref.shape[0]
    copies = []
    for i, (who, out) in enumerate(((other_ref, send_ref), (index_ref, own_ref))):
        for b in range(n):
            src = pages_ref.at[table_ref[who[b]], pl.ds(PIECE, RANK), :]
            copies.append(pltpu.make_async_copy(src, out.at[b], sems.at[i, b]))
    for c in copies:
        c.start()
    for c in copies:
        c.wait()


def choose(index, other, table, pages):
    shape = jax.ShapeDtypeStruct((index.shape[0], RANK, pages.shape[2]), pages.dtype)
    return pl.pallas_call(
        choose_kernel,
        out_shape=[shape, shape],
        in_specs=[SMEM, SMEM, SMEM, ANY],
        out_specs=[VMEM, VMEM],
        scratch_shapes=[pltpu.SemaphoreType.DMA((2, index.shape[0]))],
        compiler_params=params(8),
        cost_estimate=cost(MIB // 2),
    )(index, other, table, pages)


def total_kernel(core_ref, in_ref, up_ref, out_ref, up, sem):
    ranks = up.shape[0]
    rows = pl.ds(pl.multiple_of(core_ref[0] * ranks, ranks), ranks)
    copy = pltpu.make_async_copy(up_ref.at[0, rows, :], up, sem)
    copy.start()
    summed = jnp.sum(in_ref[...].astype(jnp.float32), axis=0).astype(out_ref.dtype)
    n, _, own = out_ref.shape
    copy.wait()
    for d in range(n):
        out_ref[d, :PIECE, :] = summed
        for i in range(CORES):
            at = PIECE + i * ranks
            out_ref[d, at : at + ranks, :] = up[:, (CORES * d + i) * own : (CORES * d + i + 1) * own]


def total(core, pieces, up):
    tp, _, own = pieces.shape
    return pl.pallas_call(
        total_kernel,
        out_shape=jax.ShapeDtypeStruct((tp, PIECE + RANK, own), pieces.dtype),
        in_specs=[SMEM, VMEM, ANY],
        out_specs=VMEM,
        scratch_shapes=[pltpu.VMEM((RANK // CORES, up.shape[2]), up.dtype), pltpu.SemaphoreType.DMA],
        compiler_params=params(8),
        cost_estimate=cost(MIB),
    )(core, pieces, up)


def product_kernel(n, parts, parity_ref, x_ref, *refs):
    offsets = [o for p in parts for o in p]
    xs, weights, outs = refs[: len(parts)], refs[len(parts) : len(parts) + n], refs[len(parts) + n : len(parts) + 2 * n]
    gathered, held, x_sems, w_sems = refs[len(parts) + 2 * n : len(parts) + 2 * n + 4]
    made, o_sems = refs[len(parts) + 2 * n + 4 : -1], refs[-1]
    leaving = [pltpu.make_async_copy(made[k], outs[k], o_sems.at[k]) for k in range(n)]
    parity = parity_ref[0]
    ny, own = held.shape[1], held.shape[2]
    at, copies = 0, []
    for i, (x, p) in enumerate(zip(xs, parts)):
        to = gathered.at[at] if len(x.shape) == 2 else gathered.at[pl.ds(at, len(p))]
        copies.append(pltpu.make_async_copy(x, to, x_sems.at[i]))
        at += len(p)
    into = []
    for k, w in enumerate(weights):
        if len(w.shape) == 3:
            into.append([pltpu.make_async_copy(w, held.at[k], w_sems.at[k, 0])])
        else:
            nx = w.shape[0] // (ny * own)
            into.append([])
            for r in range(ny):
                rows = pl.ds(pl.multiple_of((r * nx + x_ref[0]) * own, own), own)
                into[-1].append(pltpu.make_async_copy(w.at[rows, :], held.at[k, r], w_sems.at[k, r]))
    for c in (*copies, *[c for group in into for c in group]):
        c.start()
    for c in copies:
        c.wait()
    for k in range(n):
        for c in into[k]:
            c.wait()
        w = jnp.concatenate([held[k, o + (1 - parity if p else parity)] for p, o in offsets], axis=0)
        for m in range(0, gathered.shape[1], 256):
            rows = slice(m, m + 256)
            x = jnp.concatenate([gathered[j, rows, :] for j in range(ny)], axis=1)
            made[k][rows, :] = jnp.dot(x, w, preferred_element_type=jnp.float32).astype(outs[k].dtype)
        leaving[k].start()
    for c in leaving:
        c.wait()


def product(scalars, gathered, parts, weights, dtypes):
    n = len(weights)
    tokens, own = gathered[0].shape[-2:]
    ny = sum(len(p) for p in parts)
    width = weights[0].shape[-1]
    return pl.pallas_call(
        functools.partial(product_kernel, n, parts),
        out_shape=[jax.ShapeDtypeStruct((tokens, width), d) for d in dtypes],
        in_specs=[SMEM] * 2 + [ANY] * (len(gathered) + n),
        out_specs=[ANY] * n,
        scratch_shapes=[
            pltpu.VMEM((ny, tokens, own), gathered[0].dtype),
            pltpu.VMEM((n, ny, own, width), weights[0].dtype),
            pltpu.SemaphoreType.DMA((len(gathered),)),
            pltpu.SemaphoreType.DMA((n, ny)),
            *(pltpu.VMEM((tokens, width), d) for d in dtypes),
            pltpu.SemaphoreType.DMA((n,)),
        ],
        compiler_params=params(WHOLE),
        cost_estimate=cost(2 * n * MIB, 2 * tokens * ny * own * width * n),
    )(*scalars, *gathered, *weights)


def last_kernel(core_ref, low_ref, mine_ref, other_ref, own_hbm, r1_ref, r2_ref, r3_ref, out_ref, own_ref, sem):
    copy = pltpu.make_async_copy(own_hbm, own_ref, sem)
    copy.start()
    core = core_ref[0]
    half = RANK // CORES
    each = half // PIECE
    for b in range(mine_ref.shape[0]):
        rows = slice(b * BLOCK, (b + 1) * BLOCK)
        up = jnp.concatenate(
            [
                jnp.concatenate([r[b, i * half : (i + 1) * half, :] for i in range(CORES)], axis=1)
                for r in (mine_ref, other_ref)
            ],
            axis=0,
        )
        at = b * CORES * each
        shrunk = jnp.concatenate(
            [low_ref[pl.ds(at + c * each, each), :PIECE, :].reshape(half, BLOCK) for c in (core, 1 - core)], axis=0
        )
        adapted = lax.dot_general(
            shrunk, up, (((0,), (0,)), ((), ())), preferred_element_type=jnp.float32
        )
        if b == 0:
            copy.wait()
        base = own_ref[rows, :]
        for r in (r1_ref, r2_ref, r3_ref):
            base = base + r[rows, :].astype(jnp.float32)
        out_ref[rows, :] = (base + adapter_scale * adapted).astype(out_ref.dtype)


def last(core, low, mine, other, own, received):
    return pl.pallas_call(
        last_kernel,
        out_shape=jax.ShapeDtypeStruct(own.shape, jnp.bfloat16),
        in_specs=[SMEM] + [VMEM] * 3 + [ANY] + [VMEM] * 3,
        out_specs=VMEM,
        scratch_shapes=[pltpu.VMEM(own.shape, own.dtype), pltpu.SemaphoreType.DMA],
        compiler_params=params(8),
        cost_estimate=cost(3 * MIB, 2 * own.size * RANK),
    )(core, low, mine, other, own, *received)


def solution(mesh):
    tp, rep = mesh.shape["tp"], mesh.shape["rep"]
    ny, nx = NY, tp // NY
    names = ("z", "core", "yh", "yl", "x")
    grid = Mesh(mesh.devices.reshape(rep // CORES, CORES, ny // PARITIES, PARITIES, nx), names)
    reps, tps, ys = names[:2], names[2:], names[2:4]

    def shift(a, axis, size, by):
        return lax.ppermute(a, axis, [(i, (i + by) % size) for i in range(size)])

    def local(attn, weight, down, up, index, table):
        own, width = attn.shape[1], weight.shape[1]
        x, parity, core = (lax.axis_index(a).astype(jnp.int32) for a in ("x", "yl", "core"))
        scalars = (parity[None], x[None])

        pages = lax.all_to_all(pack(down, tp), tps, 0, 0, tiled=True)

        same = lax.all_gather(attn, "yh")
        pages, same = lax.optimization_barrier((pages, same))
        half = same.shape[0] // 2
        low_y = shift(same[:half], ys, ny, 1)
        high_y = shift(same[half:], ys, ny, -1)
        gathered = (same, low_y, high_y)
        parts = tuple(
            tuple((p, PARITIES * h) for h in hs)
            for p, hs in ((0, range(2 * half)), (1, range(half)), (1, range(half, 2 * half)))
        )

        by_x = weight.reshape(ny, nx, own, width)
        ws = [
            lax.dynamic_index_in_dim(by_x, (x + (nx - k)) % nx, 1, keepdims=False)
            for k in range(1, nx)
        ]
        ws = [shift(w, "x", nx, nx - k) for k, w in enumerate(ws, 1)]

        pieces = shrink(index, table, attn, pages)
        pieces = lax.all_to_all(pieces, tps, 0, 0, tiled=True)

        *outs, mid = product(
            scalars, gathered, parts, [*ws, weight], [jnp.bfloat16] * len(ws) + [jnp.float32]
        )
        pieces = lax.optimization_barrier((pieces, outs))[0]
        summed = total(core[None], pieces, up)
        low = lax.all_to_all(summed, tps, 0, 0, tiled=True)
        received = [shift(o, "x", nx, k) for k, o in enumerate(outs, 1)]

        index, _ = lax.optimization_barrier((index, (summed, outs)))
        other_index = shift(index, "core", CORES, 1)
        mine, send = choose(index, other_index, table, low)
        other = shift(send, "core", CORES, 1)
        return last(core[None], low, mine, other, mid, received)

    return jax.shard_map(
        local,
        mesh=grid,
        in_specs=(P(reps, tps), P(None, tps), P(tps), P(tps), P(reps), P()),
        out_specs=P(reps, tps),
        check_vma=False,
    )
```
